32 devices in a mesh: grp: 4 (over x, core), mem: 4 (over z), pair: 2 (over y).
Axes of the slice: x: 2, y: 2, z: 4, core: 2. Of those that a mesh axis runs over, the one named last changes fastest.
Arguments:
- voltages: bfloat16 [1024, 2, 71680], P(('grp', 'mem'), 'pair'), may hold values from -6 to 6
- gain_table: float32 [64, 2, 1024], P(None, None, 'mem'), may hold values from -4.2 to 4.2
- gain_index: int32 [1024, 2], replicated, may hold values from 0 to 63
- cylinder_map: int32 [1024], replicated, may hold values from 0 to 1023, each once
- delays: int32 [32, 1024], replicated, may hold values from 0 to 31
- chan_map: int32 [1024], replicated, may hold values from 0 to 1023, each once
Outputs:
- dedispersed: float32 [2, 512, 32, 32], P('pair', ('grp', 'mem'))
The draws below stay inside these ranges and needn't reach their ends.
Inputs may be any that keep to these rules, and one draw needn't show every extreme that they name: `cylinder_map`: each of 0 to 1023 appears once. `chan_map`: each of 0 to 1023 appears once.
All inputs are finite; a program needn't handle non-finite values.
Results may differ from the reference program's by a relative error of at most 0.011.
Values may be sent and summed in bfloat16 or wider, within the bound.
A program may use at most 128 MiB of HBM per device.

```python
import math
import jax
import jax.numpy as jnp
from jax import lax

NFFT = 2048
CHANS = 1024
TAPS = 4
CYL = 4
NS = 256
POLS = 2
FEEDS = 1024
BEAMS = 1024
TIMES = 32
SAMPLES = 71680
TRIALS = 32
GAIN_ROWS = 64


def touch_ends(result, key, low, top_value):
    longest = result.shape.index(max(result.shape))
    spots = []
    for shift in (0, 1):
        where = [jax.random.randint(jax.random.fold_in(key, axis), (), 0, length) for axis, length in enumerate(result.shape)]
        where[longest] = (where[longest] + shift) % result.shape[longest]
        spots.append(tuple(where))
    return result.at[spots[0]].set(low).at[spots[1]].set(top_value)


def level_of(key, shape, cuts, low, largest):
    gain = 1.0
    for dim, shards_of in cuts:
        heights = jax.random.uniform(jax.random.fold_in(jax.random.fold_in(key, 6), dim), (shards_of,), jnp.float32, low / len(cuts), largest / len(cuts))
        gain = gain * jnp.repeat(jnp.exp(heights), shape[dim] // shards_of).reshape((-1,) + (1,) * (len(shape) - 1 - dim))
    return gain


def noise(stream_key, dims, scale, limit, split=(), held_as=jnp.bfloat16):
    factor_of = level_of(stream_key, dims, split, -0.22, 0.18) if split else 1.0
    entries = jax.random.normal(stream_key, dims, jnp.float32) * scale * factor_of
    return jnp.minimum(jnp.maximum(entries, -limit), limit).astype(held_as)


def setup_inputs(seed: int = 0) -> dict:
    seeds = jax.random.split(jax.random.key(seed), 7)
    voltages = noise(seeds[0], (FEEDS, POLS, SAMPLES), 1.0, 6.0, ((0, 16), (1, 2)))
    gain_table = noise(seeds[1], (GAIN_ROWS, 2, CHANS), 0.7, 4.2, ((2, 4),), jnp.float32)
    gain_index = touch_ends(jax.random.randint(seeds[2], (FEEDS, POLS), 0, GAIN_ROWS), jax.random.fold_in(seeds[2], 1), 0, GAIN_ROWS - 1).astype(jnp.int32)
    cylinder_map = jax.random.permutation(seeds[3], FEEDS).astype(jnp.int32)
    delays = touch_ends(jax.random.randint(seeds[4], (TRIALS, CHANS), 0, TIMES), jax.random.fold_in(seeds[4], 1), 0, TIMES - 1).astype(jnp.int32)
    chan_map = jax.random.permutation(seeds[5], CHANS).astype(jnp.int32)
    return {"voltages": voltages, "gain_table": gain_table, "gain_index": gain_index, "cylinder_map": cylinder_map, "delays": delays, "chan_map": chan_map}


HIGHEST_PRECISION = lax.Precision.HIGHEST

def pfb_window(tap_count, length):
    offsets = jnp.arange(tap_count * length, dtype=jnp.float32) + 0.5
    shaped = jnp.sinc((offsets - tap_count * length / 2.0) / length)
    taper_term = 0.5 - 0.5 * jnp.cos(offsets * (2.0 * math.pi / (tap_count * length)))
    return (shaped * taper_term).reshape(tap_count, length)

def channel_table(length, start_col, columns):
    samples = jnp.arange(length, dtype=jnp.int32)[:, None]
    channels = start_col + jnp.arange(columns, dtype=jnp.int32)[None, :]
    turns_int = samples * channels % length
    angles = turns_int.astype(jnp.float32) * (2.0 * math.pi / length)
    return (jnp.cos(angles).astype(jnp.bfloat16), (-jnp.sin(angles)).astype(jnp.bfloat16))

def frame_signal(volt_rows, window):
    leading = volt_rows.shape[0]
    frames = volt_rows.reshape(leading, TIMES + TAPS - 1, NFFT).astype(jnp.float32)
    framed = frames[:, 0:TIMES] * window[0]
    for tap_index in range(1, TAPS):
        framed = framed + frames[:, tap_index:tap_index + TIMES] * window[tap_index]
    return framed.astype(jnp.bfloat16).reshape(leading * TIMES, NFFT)

def beam_table(length):
    samples = jnp.arange(length, dtype=jnp.int32).reshape(length, 1, 1)
    beam_index = jnp.arange(length, dtype=jnp.int32).reshape(length // 2, 2).T.reshape(1, 2, length // 2)
    turns_int = samples * beam_index % length
    angles = turns_int.astype(jnp.float32) * (2.0 * math.pi / length)
    cosine = jnp.cos(angles).astype(jnp.bfloat16)
    sine_part = jnp.sin(angles).astype(jnp.bfloat16)
    first_row = jnp.stack([cosine, -sine_part], axis=1)
    second_row = jnp.stack([sine_part, cosine], axis=1)
    return jnp.stack([first_row, second_row], axis=1)

def beam_power(ns_real, ns_imag, feed_total):
    cylinders = ns_real.shape[1]
    indices = jnp.arange(cylinders, dtype=jnp.int32)
    turns_int = indices[:, None] * indices[None, :] % cylinders
    angles = turns_int.astype(jnp.float32) * (2.0 * math.pi / cylinders)
    cosine = jnp.cos(angles)
    sine_table = jnp.sin(angles)
    beam_real = jnp.einsum('ec,lchq->lehq', cosine, ns_real, precision=HIGHEST_PRECISION) + jnp.einsum('ec,lchq->lehq', sine_table, ns_imag, precision=HIGHEST_PRECISION)
    beam_imag = jnp.einsum('ec,lchq->lehq', cosine, ns_imag, precision=HIGHEST_PRECISION) - jnp.einsum('ec,lchq->lehq', sine_table, ns_real, precision=HIGHEST_PRECISION)
    return (beam_real * beam_real + beam_imag * beam_imag) * (1.0 / feed_total)

def time_tables(length):
    indices = jnp.arange(length, dtype=jnp.int32)
    turns_int = indices[:, None] * indices[None, :] % length
    angles = turns_int.astype(jnp.float32) * (2.0 * math.pi / length)
    return (jnp.cos(angles), jnp.sin(angles))

def dedisperse(intensity, delays, chan_map):
    values = intensity.astype(jnp.float32)
    centred = values - lax.optimization_barrier(jnp.mean(values, axis=1, keepdims=True))
    cosine, sine_table = time_tables(TIMES)
    spec_real = jnp.einsum('btc,tk->bkc', centred, cosine, precision=HIGHEST_PRECISION).astype(jnp.bfloat16)
    spec_imag = (-jnp.einsum('btc,tk->bkc', centred, sine_table, precision=HIGHEST_PRECISION)).astype(jnp.bfloat16)
    trial_delay = jnp.take(delays, chan_map, axis=1)
    wave_index = jnp.arange(TIMES, dtype=jnp.int32)
    turns_int = wave_index[:, None, None] * trial_delay[None] % TIMES
    angles = turns_int.astype(jnp.float32) * (2.0 * math.pi / TIMES)
    phase_real = jnp.cos(angles).astype(jnp.bfloat16).astype(jnp.float32)
    phase_imag = (-jnp.sin(angles)).astype(jnp.bfloat16).astype(jnp.float32)
    spec_real = spec_real.astype(jnp.float32)
    spec_imag = spec_imag.astype(jnp.float32)
    trial_real = jnp.einsum('bkc,kjc->bkj', spec_real, phase_real, precision=HIGHEST_PRECISION) - jnp.einsum('bkc,kjc->bkj', spec_imag, phase_imag, precision=HIGHEST_PRECISION)
    trial_imag = jnp.einsum('bkc,kjc->bkj', spec_real, phase_imag, precision=HIGHEST_PRECISION) + jnp.einsum('bkc,kjc->bkj', spec_imag, phase_real, precision=HIGHEST_PRECISION)
    scale_out = 1.0 / (TIMES * math.sqrt(CHANS))
    series = jnp.einsum('bkj,kt->bjt', trial_real, cosine, precision=HIGHEST_PRECISION) - jnp.einsum('bkj,kt->bjt', trial_imag, sine_table, precision=HIGHEST_PRECISION)
    return series * scale_out

def reference(voltages, gain_table, gain_index, cylinder_map, delays, chan_map):
    window = pfb_window(TAPS, NFFT)
    cos_table, sin_table = channel_table(NFFT, 0, CHANS)
    scale_dft = 1.0 / math.sqrt(NFFT)
    group_size = 32
    grouped = voltages.reshape(FEEDS // group_size, group_size * POLS, SAMPLES)

    def channelize(volt_rows):
        framed = frame_signal(volt_rows, window)
        real_part = jnp.dot(framed, cos_table, preferred_element_type=jnp.float32) * scale_dft
        imag_part = jnp.dot(framed, sin_table, preferred_element_type=jnp.float32) * scale_dft
        stacked = jnp.stack([real_part, imag_part], axis=0).astype(jnp.bfloat16)
        return stacked.reshape(2, group_size * POLS, TIMES, CHANS)
    spectra = lax.map(channelize, grouped)
    spectra = jnp.moveaxis(spectra, 1, 0).reshape(2, FEEDS, POLS, TIMES, CHANS)
    ordered = jnp.take(spectra, cylinder_map, axis=1)
    ordered = jnp.moveaxis(ordered, 3, 0)
    gain_rows = jnp.take(gain_index, cylinder_map, axis=0)
    gain_values = jnp.take(gain_table, gain_rows, axis=0)
    gain_real = gain_values[:, :, 0]
    gain_imag = gain_values[:, :, 1]
    ns_table = beam_table(NS).astype(jnp.float32)

    def form_beams(time_slab):
        volt_real = time_slab[0].astype(jnp.float32)
        volt_imag = time_slab[1].astype(jnp.float32)
        cal_real = volt_real * gain_real - volt_imag * gain_imag
        cal_imag = volt_real * gain_imag + volt_imag * gain_real
        cal_grid = lax.optimization_barrier(jnp.stack([cal_real, cal_imag], axis=0).astype(jnp.bfloat16))
        cal_grid = cal_grid.astype(jnp.float32).reshape(2, CYL, NS, POLS, CHANS)
        ns_beams = jnp.einsum('rcnpl,nrsah->spachl', cal_grid, ns_table, precision=HIGHEST_PRECISION)
        half_beams = NS // 2
        powers = beam_power(ns_beams[0].reshape(POLS * 2, CYL, half_beams, CHANS), ns_beams[1].reshape(POLS * 2, CYL, half_beams, CHANS), FEEDS)
        powers = powers.reshape(POLS, 2, CYL, half_beams, CHANS)
        return (powers[0] + powers[1]).astype(jnp.bfloat16)
    intensity = lax.map(form_beams, ordered)
    intensity = jnp.transpose(intensity, (1, 2, 3, 0, 4)).reshape(BEAMS, TIMES, CHANS)
    series = dedisperse(intensity, delays, chan_map)
    return series.reshape(2, BEAMS // 2, TRIALS, TIMES)
```

```python
import functools
import math

import jax
import jax.numpy as jnp
from jax import lax
from jax.experimental import pallas as pl
from jax.experimental.pallas import tpu as pltpu
from jax.sharding import PartitionSpec as P

NFFT = 2048
CHANS = 1024
TAPS = 4
CYL = 4
NS = 256
FEEDS = 1024
BEAMS = 1024
TIMES = 32
TRIALS = 32
PEERS = ("grp", "mem")
LANES = 128


def pfb_window(tap_count, length):
    offsets = jnp.arange(tap_count * length, dtype=jnp.float32) + 0.5
    shaped = jnp.sinc((offsets - tap_count * length / 2.0) / length)
    taper_term = 0.5 - 0.5 * jnp.cos(offsets * (2.0 * math.pi / (tap_count * length)))
    return (shaped * taper_term).reshape(tap_count, length)


def turn(index, length):
    angles = (index % length).astype(jnp.float32) * (2.0 * math.pi / length)
    return lax.optimization_barrier((jnp.cos(angles), jnp.sin(angles)))


def times(a, b):
    return (a[0] * b[0] - a[1] * b[1], a[0] * b[1] + a[1] * b[0])


def channel_table(chan_of, quarter):
    chan = chan_of[None, :]
    high = turn(jnp.arange(16, dtype=jnp.int32)[:, None] * 128 * chan, NFFT)
    mid = turn(jnp.arange(16, dtype=jnp.int32)[:, None] * 8 * chan, NFFT)
    low = turn(jnp.arange(8, dtype=jnp.int32)[:, None] * chan + quarter[None, :] * (NFFT // 4), NFFT)
    upper = times([p[:, None, :] for p in high], [p[None, :, :] for p in mid])
    upper = lax.optimization_barrier(tuple(p.reshape(NFFT // 8, 1, -1) for p in upper))
    table = upper[0] * low[0][None] - upper[1] * low[1][None]
    return table.astype(jnp.bfloat16).reshape(NFFT, -1)


def beam_weights(cylinder_map):
    slots = jnp.arange(FEEDS, dtype=jnp.int32)
    hit = cylinder_map[:, None] == slots[None, :]
    slot_of = jnp.sum(jnp.where(hit, slots[:, None], 0), axis=0)
    cyl, pos = slot_of // NS, slot_of % NS
    e = jnp.arange(CYL, dtype=jnp.int32).reshape(CYL, 1, 1)
    hh = jnp.arange(16, dtype=jnp.int32).reshape(1, 16, 1)
    upper = turn(16 * pos * hh + (NS // CYL) * e * cyl, NS)
    a = jnp.arange(2, dtype=jnp.int32).reshape(2, 1, 1)
    hl = jnp.arange(8, dtype=jnp.int32).reshape(1, 8, 1)
    lower = turn(pos * (2 * hl + a), NS)
    real, imag = times(
        [p[None, :, :, None, :] for p in upper], [p[:, None, None, :, :] for p in lower]
    )
    return jnp.concatenate(
        [p.astype(jnp.bfloat16).reshape(BEAMS, FEEDS) for p in (real, imag)], axis=1
    )


def frame_signal(volt_rows, window):
    leading = volt_rows.shape[0]
    frames = volt_rows.reshape(leading, TIMES + TAPS - 1, NFFT).astype(jnp.float32)
    framed = frames[:, 0:TIMES] * window[0]
    for tap_index in range(1, TAPS):
        framed = framed + frames[:, tap_index : tap_index + TIMES] * window[tap_index]
    return framed.astype(jnp.bfloat16)


HIT = (TIMES - 1) / (TIMES * TIMES)
MISS = -1.0 / (TIMES * TIMES)


def beam_kernel(block, chans, r_ref, ga_ref, gb_ref, w_ref, e_ref, out_ref, x_ref, t_ref, p_ref):
    step = pl.program_id(0)
    width = 2 * chans
    lane = lax.broadcasted_iota(jnp.int32, (FEEDS, width), 1)
    sign = jnp.where(lane < chans, 1.0, -1.0)
    for i in range(block):
        volt = r_ref[:, i].reshape(FEEDS, width).astype(jnp.float32)
        cal = volt * ga_ref[...] + pltpu.roll(volt, chans, 1) * gb_ref[...]
        turned = pltpu.roll(cal, chans, 1) * sign
        cols = slice(i * width, (i + 1) * width)
        x_ref[0:FEEDS, cols] = cal.astype(jnp.bfloat16)
        x_ref[FEEDS : 2 * FEEDS, cols] = turned.astype(jnp.bfloat16)
        hit = e_ref[...] == step * block + i
        t_ref[i * chans : (i + 1) * chans, :] = jnp.where(hit, HIT, MISS).astype(jnp.bfloat16)
    low = lax.broadcasted_iota(jnp.int32, (BEAMS, width), 1) < chans
    for i in range(0, block, 2):
        cols = slice(i * width, (i + 2) * width)
        beams = jnp.dot(w_ref[...], x_ref[:, cols], preferred_element_type=jnp.float32)
        squares = beams * beams
        one, two = squares[:, :width], squares[:, width:]
        first = one + pltpu.roll(one, chans, 1)
        second = two + pltpu.roll(two, chans, 1)
        power = jnp.where(low, first, second) * (1.0 / FEEDS)
        p_ref[:, i * chans : (i + 2) * chans] = power.astype(jnp.bfloat16)
    part = jnp.dot(p_ref[...], t_ref[...], preferred_element_type=jnp.float32)

    @pl.when(step == 0)
    def _():
        out_ref[...] = part

    @pl.when(step > 0)
    def _():
        out_ref[...] += part


def beam_stage(received, gains, weights, shift):
    peers, _, feeds, width = received.shape
    chans = width // 2
    if width != LANES:
        volt = jnp.moveaxis(received, 1, 0).reshape(TIMES, FEEDS, 2, chans).astype(jnp.float32)
        ga, gb = (g.reshape(FEEDS, 2, chans) for g in gains)
        cal = (volt * ga + volt[:, :, ::-1] * gb).astype(jnp.bfloat16)
        turned = jnp.stack([cal[:, :, 1], -cal[:, :, 0]], axis=2)
        both = jnp.concatenate([cal, turned], axis=1)
        beams = jnp.einsum("bf,tfrc->btrc", weights, both, preferred_element_type=jnp.float32)
        power = jnp.sum(beams * beams, axis=2) * (1.0 / FEEDS)
        power = power.astype(jnp.bfloat16).reshape(BEAMS, TIMES * chans)
        hit = shift[None] == jnp.arange(TIMES, dtype=jnp.int32)[:, None, None]
        spread = jnp.where(hit, HIT, MISS).astype(jnp.bfloat16).reshape(TIMES * chans, -1)
        return jnp.dot(power, spread, preferred_element_type=jnp.float32)
    block = 8
    series = TRIALS * TIMES
    whole = lambda shape: pl.BlockSpec(shape, lambda i: (0,) * len(shape))
    return pl.pallas_call(
        functools.partial(beam_kernel, block, chans),
        grid=(TIMES // block,),
        out_shape=jax.ShapeDtypeStruct((BEAMS, series), jnp.float32),
        in_specs=[
            pl.BlockSpec((peers, block, feeds, width), lambda i: (0, i, 0, 0)),
            whole((FEEDS, width)),
            whole((FEEDS, width)),
            whole((BEAMS, 2 * FEEDS)),
            whole((chans, series)),
        ],
        out_specs=whole((BEAMS, series)),
        scratch_shapes=[
            pltpu.VMEM((2 * FEEDS, block * width), jnp.bfloat16),
            pltpu.VMEM((block * chans, series), jnp.bfloat16),
            pltpu.VMEM((BEAMS, block * chans), jnp.bfloat16),
        ],
        compiler_params=pltpu.CompilerParams(
            dimension_semantics=("arbitrary",), vmem_limit_bytes=60 * 1024 * 1024
        ),
    )(received, *gains, weights, shift)


def local(voltages, gain_table, gain_index, cylinder_map, delays, chan_map):
    feeds = voltages.shape[0]
    grp_count, mem_count = lax.axis_size("grp"), lax.axis_size("mem")
    peers = grp_count * mem_count
    chans = CHANS // peers
    grp, mem = lax.axis_index("grp"), lax.axis_index("mem")

    window = pfb_window(TAPS, NFFT)
    framed = frame_signal(voltages.reshape(feeds, voltages.shape[2]), window)
    peer = jnp.arange(peers, dtype=jnp.int32)
    base = peer % mem_count * (CHANS // mem_count) + peer // mem_count * chans
    chan_of = base[:, None, None] + jnp.arange(chans, dtype=jnp.int32)[None, None, :]
    quarter = jnp.arange(2, dtype=jnp.int32)[None, :, None]
    chan_of, quarter = (
        jnp.broadcast_to(v, (peers, 2, chans)).reshape(-1) for v in (chan_of, quarter)
    )
    table = channel_table(chan_of, quarter)

    rows = jnp.swapaxes(framed, 0, 1).reshape(TIMES * feeds, NFFT)
    spectra = jnp.dot(rows, table, preferred_element_type=jnp.float32) * (1.0 / math.sqrt(NFFT))
    spectra = spectra.astype(jnp.bfloat16).reshape(TIMES, feeds, peers, 2 * chans)
    spectra = jnp.moveaxis(spectra, 2, 0)
    received = lax.all_to_all(spectra, PEERS, split_axis=0, concat_axis=0, tiled=True)

    weights = beam_weights(cylinder_map)
    gain_here = lax.dynamic_slice_in_dim(gain_table, grp * chans, chans, 2)
    gain_rows = gain_index[:, lax.axis_index("pair")]
    pick = gain_rows[:, None] == jnp.arange(gain_table.shape[0], dtype=jnp.int32)[None, :]
    gain_values = jnp.dot(
        pick.astype(jnp.float32),
        gain_here.reshape(gain_table.shape[0], 2 * chans),
        precision=lax.Precision.HIGHEST,
    )
    gain_real, gain_imag = gain_values[:, :chans], gain_values[:, chans:]
    gains = (
        jnp.concatenate([gain_real, gain_real], axis=1),
        jnp.concatenate([-gain_imag, gain_imag], axis=1),
    )

    first = mem * (CHANS // mem_count) + grp * chans
    freq = lax.dynamic_slice_in_dim(chan_map, first, chans, 0)
    column = jnp.arange(CHANS, dtype=jnp.int32)[:, None] == freq[None, :]
    delay = jnp.dot(
        delays.astype(jnp.bfloat16), column.astype(jnp.bfloat16), preferred_element_type=jnp.float32
    ).astype(jnp.int32)
    frame = jnp.arange(TIMES, dtype=jnp.int32)[None, None, :]
    shift = ((frame - delay.T[:, :, None]) % TIMES).reshape(chans, TRIALS * TIMES)

    part = beam_stage(received, gains, weights, shift)

    pairs = lax.axis_size("pair")
    owned = BEAMS // (pairs * peers)
    part = part.astype(jnp.bfloat16).reshape(pairs * peers, owned, TRIALS * TIMES)
    parts = lax.all_to_all(part, ("pair",) + PEERS, split_axis=0, concat_axis=0, tiled=True)
    series = jnp.sum(parts.astype(jnp.float32), axis=0)
    return series.reshape(1, owned, TRIALS, TIMES)


def solution(mesh):
    return jax.shard_map(
        local,
        mesh=mesh,
        in_specs=(P(PEERS, "pair", None), P(None, None, "mem"), P(), P(), P(), P()),
        out_specs=P("pair", PEERS, None, None),
        check_vma=False,
    )
```

```python
import functools
import math

import jax
import jax.numpy as jnp
from jax import lax
from jax.experimental import pallas as pl
from jax.experimental.pallas import tpu as pltpu
from jax.sharding import PartitionSpec as P

NFFT = 2048
CHANS = 1024
TAPS = 4
CYL = 4
NS = 256
FEEDS = 1024
BEAMS = 1024
TIMES = 32
TRIALS = 32
PEERS = ("grp", "mem")
LANES = 128


def pfb_window(tap_count, length):
    offsets = jnp.arange(tap_count * length, dtype=jnp.float32) + 0.5
    shaped = jnp.sinc((offsets - tap_count * length / 2.0) / length)
    taper_term = 0.5 - 0.5 * jnp.cos(offsets * (2.0 * math.pi / (tap_count * length)))
    return (shaped * taper_term).reshape(tap_count, length)


def turn(index, length):
    angles = (index % length).astype(jnp.float32) * (2.0 * math.pi / length)
    return lax.optimization_barrier((jnp.cos(angles), jnp.sin(angles)))


def times(a, b):
    return (a[0] * b[0] - a[1] * b[1], a[0] * b[1] + a[1] * b[0])


def channel_table(chan_of, quarter):
    chan = chan_of[None, :]
    high = turn(jnp.arange(16, dtype=jnp.int32)[:, None] * 128 * chan, NFFT)
    mid = turn(jnp.arange(16, dtype=jnp.int32)[:, None] * 8 * chan, NFFT)
    low = turn(jnp.arange(8, dtype=jnp.int32)[:, None] * chan + quarter[None, :] * (NFFT // 4), NFFT)
    upper = times([p[:, None, :] for p in high], [p[None, :, :] for p in mid])
    upper = lax.optimization_barrier(tuple(p.reshape(NFFT // 8, 1, -1) for p in upper))
    table = upper[0] * low[0][None] - upper[1] * low[1][None]
    return table.astype(jnp.bfloat16).reshape(NFFT, -1)


def beam_weights(cylinder_map):
    slots = jnp.arange(FEEDS, dtype=jnp.int32)
    hit = cylinder_map[:, None] == slots[None, :]
    slot_of = jnp.sum(jnp.where(hit, slots[:, None], 0), axis=0)
    cyl, pos = slot_of // NS, slot_of % NS
    e = jnp.arange(CYL, dtype=jnp.int32).reshape(CYL, 1, 1)
    hh = jnp.arange(16, dtype=jnp.int32).reshape(1, 16, 1)
    upper = turn(16 * pos * hh + (NS // CYL) * e * cyl, NS)
    a = jnp.arange(2, dtype=jnp.int32).reshape(2, 1, 1)
    hl = jnp.arange(8, dtype=jnp.int32).reshape(1, 8, 1)
    lower = turn(pos * (2 * hl + a), NS)
    real, imag = times(
        [p[None, :, :, None, :] for p in upper], [p[:, None, None, :, :] for p in lower]
    )
    return jnp.concatenate(
        [p.astype(jnp.bfloat16).reshape(BEAMS, FEEDS) for p in (real, imag)], axis=1
    )


CHUNKS = (4, 12, 12, 4)


def dft_kernel(frames, feeds, window_ref, volt_ref, table_ref, out_ref, framed_ref):
    @pl.when(pl.program_id(0) == 0)
    def _():
        for t in range(frames):
            total = volt_ref[:, t * NFFT : (t + 1) * NFFT].astype(jnp.float32) * window_ref[0:1, :]
            for j in range(1, TAPS):
                tap = volt_ref[:, (t + j) * NFFT : (t + j + 1) * NFFT].astype(jnp.float32)
                total = total + tap * window_ref[j : j + 1, :]
            framed_ref[t * feeds : (t + 1) * feeds, :] = total.astype(jnp.bfloat16)

    part = jnp.dot(framed_ref[...], table_ref[...], preferred_element_type=jnp.float32)
    part = (part * (1.0 / math.sqrt(NFFT))).astype(jnp.bfloat16)
    for i in range(out_ref.shape[0]):
        out_ref[i] = part[:, i * LANES : (i + 1) * LANES].reshape(frames, feeds, LANES)


def dft_stage(voltages, window, table, start, frames, peers):
    feeds = voltages.shape[0]
    length = (frames + TAPS - 1) * NFFT
    volt = lax.slice_in_dim(voltages, start * NFFT, start * NFFT + length, axis=2)
    volt = volt.reshape(feeds, length)
    width = table.shape[1] // peers
    if width != LANES:
        view = volt.reshape(feeds, frames + TAPS - 1, NFFT).astype(jnp.float32)
        framed = view[:, 0:frames] * window[0]
        for j in range(1, TAPS):
            framed = framed + view[:, j : j + frames] * window[j]
        rows = jnp.swapaxes(framed.astype(jnp.bfloat16), 0, 1).reshape(frames * feeds, NFFT)
        part = jnp.dot(rows, table, preferred_element_type=jnp.float32) * (1.0 / math.sqrt(NFFT))
        part = part.astype(jnp.bfloat16).reshape(frames, feeds, peers, width)
        return jnp.moveaxis(part, 2, 0)
    step = 4
    return pl.pallas_call(
        functools.partial(dft_kernel, frames, feeds),
        grid=(peers // step,),
        out_shape=jax.ShapeDtypeStruct((peers, frames, feeds, width), jnp.bfloat16),
        in_specs=[
            pl.BlockSpec((TAPS, NFFT), lambda i: (0, 0)),
            pl.BlockSpec((feeds, length), lambda i: (0, 0)),
            pl.BlockSpec((NFFT, step * width), lambda i: (0, i)),
        ],
        out_specs=pl.BlockSpec((step, frames, feeds, width), lambda i: (i, 0, 0, 0)),
        scratch_shapes=[pltpu.VMEM((frames * feeds, NFFT), jnp.bfloat16)],
        compiler_params=pltpu.CompilerParams(
            dimension_semantics=("arbitrary",), vmem_limit_bytes=56 * 1024 * 1024
        ),
    )(window, volt, table)


HIT = (TIMES - 1) / (TIMES * TIMES)
MISS = -1.0 / (TIMES * TIMES)


def beam_kernel(start, frames, chans, r_ref, ga_ref, gb_ref, w_ref, e_ref, *rest):
    acc_ref = rest[0] if len(rest) == 5 else None
    out_ref, x_ref, t_ref, p_ref = rest[-4:]
    width = 2 * chans
    lane = lax.broadcasted_iota(jnp.int32, (FEEDS, width), 1)
    sign = jnp.where(lane < chans, 1.0, -1.0)
    low = lax.broadcasted_iota(jnp.int32, (BEAMS, width), 1) < chans

    def calibrate(i, carry):
        volt = r_ref[:, i].reshape(FEEDS, width).astype(jnp.float32)
        cal = volt * ga_ref[...] + pltpu.roll(volt, chans, 1) * gb_ref[...]
        turned = pltpu.roll(cal, chans, 1) * sign
        cols = pl.ds(pl.multiple_of(i * width, width), width)
        x_ref[0:FEEDS, cols] = cal.astype(jnp.bfloat16)
        x_ref[FEEDS : 2 * FEEDS, cols] = turned.astype(jnp.bfloat16)
        hit = e_ref[...] == start + i
        rows = pl.ds(pl.multiple_of(i * chans, chans), chans)
        t_ref[rows, :] = jnp.where(hit, HIT, MISS).astype(jnp.bfloat16)
        return carry

    def form(i, carry):
        cols = pl.ds(pl.multiple_of(i * 2 * width, 2 * width), 2 * width)
        beams = jnp.dot(w_ref[...], x_ref[:, cols], preferred_element_type=jnp.float32)
        squares = beams * beams
        one, two = squares[:, :width], squares[:, width:]
        first = one + pltpu.roll(one, chans, 1)
        second = two + pltpu.roll(two, chans, 1)
        power = jnp.where(low, first, second) * (1.0 / FEEDS)
        p_ref[:, pl.ds(pl.multiple_of(i * width, width), width)] = power.astype(jnp.bfloat16)
        return carry

    lax.fori_loop(0, frames, calibrate, 0)
    lax.fori_loop(0, frames // 2, form, 0)
    part = jnp.dot(p_ref[...], t_ref[...], preferred_element_type=jnp.float32)
    if acc_ref is not None:
        part = part + acc_ref[...]
    out_ref[...] = part.astype(out_ref.dtype)


def beam_stage(received, gains, weights, shift, start, acc):
    _, frames, _, width = received.shape
    chans = width // 2
    last = start + frames == TIMES
    held = jnp.bfloat16 if last else jnp.float32
    if width != LANES:
        volt = jnp.moveaxis(received, 1, 0).reshape(frames, FEEDS, 2, chans).astype(jnp.float32)
        ga, gb = (g.reshape(FEEDS, 2, chans) for g in gains)
        cal = (volt * ga + volt[:, :, ::-1] * gb).astype(jnp.bfloat16)
        turned = jnp.stack([cal[:, :, 1], -cal[:, :, 0]], axis=2)
        both = jnp.concatenate([cal, turned], axis=1)
        beams = jnp.einsum("bf,tfrc->btrc", weights, both, preferred_element_type=jnp.float32)
        power = jnp.sum(beams * beams, axis=2) * (1.0 / FEEDS)
        power = power.astype(jnp.bfloat16).reshape(BEAMS, frames * chans)
        frame = start + jnp.arange(frames, dtype=jnp.int32)[:, None, None]
        spread = jnp.where(shift[None] == frame, HIT, MISS).astype(jnp.bfloat16)
        spread = spread.reshape(frames * chans, -1)
        part = jnp.dot(power, spread, preferred_element_type=jnp.float32)
        return (part if acc is None else part + acc).astype(held)
    series = TRIALS * TIMES
    operands = (received, *gains, weights, shift) + (() if acc is None else (acc,))
    return pl.pallas_call(
        functools.partial(beam_kernel, start, frames, chans),
        out_shape=jax.ShapeDtypeStruct((BEAMS, series), held),
        in_specs=[pl.BlockSpec(memory_space=pltpu.VMEM)] * len(operands),
        out_specs=pl.BlockSpec(memory_space=pltpu.VMEM),
        scratch_shapes=[
            pltpu.VMEM((2 * FEEDS, frames * width), jnp.bfloat16),
            pltpu.VMEM((frames * chans, series), jnp.bfloat16),
            pltpu.VMEM((BEAMS, frames * chans), jnp.bfloat16),
        ],
        compiler_params=pltpu.CompilerParams(vmem_limit_bytes=56 * 1024 * 1024),
    )(*operands)


def local(voltages, gain_table, gain_index, cylinder_map, delays, chan_map):
    feeds = voltages.shape[0]
    grp_count, mem_count = lax.axis_size("grp"), lax.axis_size("mem")
    peers = grp_count * mem_count
    chans = CHANS // peers
    grp, mem = lax.axis_index("grp"), lax.axis_index("mem")

    window = pfb_window(TAPS, NFFT)
    peer = jnp.arange(peers, dtype=jnp.int32)
    base = peer % mem_count * (CHANS // mem_count) + peer // mem_count * chans
    chan_of = base[:, None, None] + jnp.arange(chans, dtype=jnp.int32)[None, None, :]
    quarter = jnp.arange(2, dtype=jnp.int32)[None, :, None]
    chan_of, quarter = (
        jnp.broadcast_to(v, (peers, 2, chans)).reshape(-1) for v in (chan_of, quarter)
    )
    table = channel_table(chan_of, quarter)

    table = lax.optimization_barrier(table)
    starts = [sum(CHUNKS[:i]) for i in range(len(CHUNKS))]

    def exchange(spectra):
        return lax.all_to_all(spectra, PEERS, split_axis=0, concat_axis=0, tiled=True)

    spectra = [
        dft_stage(voltages, window, table, start, frames, peers)
        for start, frames in zip(starts, CHUNKS)
    ]
    received = [exchange(block) for block in spectra[:-1]]

    pairs = lax.axis_size("pair")
    cores = 2 if grp_count % 2 == 0 else 1
    owned = BEAMS // (pairs * peers)
    weights = beam_weights(cylinder_map)
    weights = weights.reshape(pairs, grp_count // cores, cores, mem_count * owned, 2 * FEEDS)
    weights = jnp.moveaxis(weights, 2, 0).reshape(BEAMS, 2 * FEEDS)
    gain_here = lax.dynamic_slice_in_dim(gain_table, grp * chans, chans, 2)
    gain_rows = gain_index[:, lax.axis_index("pair")]
    pick = gain_rows[:, None] == jnp.arange(gain_table.shape[0], dtype=jnp.int32)[None, :]
    gain_values = jnp.dot(
        pick.astype(jnp.float32),
        gain_here.reshape(gain_table.shape[0], 2 * chans),
        precision=lax.Precision.HIGHEST,
    )
    gain_real, gain_imag = gain_values[:, :chans], gain_values[:, chans:]
    gains = (
        jnp.concatenate([gain_real, gain_real], axis=1),
        jnp.concatenate([-gain_imag, gain_imag], axis=1),
    )

    first = mem * (CHANS // mem_count) + grp * chans
    freq = lax.dynamic_slice_in_dim(chan_map, first, chans, 0)
    column = jnp.arange(CHANS, dtype=jnp.int32)[:, None] == freq[None, :]
    delay = jnp.dot(
        delays.astype(jnp.bfloat16), column.astype(jnp.bfloat16), preferred_element_type=jnp.float32
    ).astype(jnp.int32)
    frame = jnp.arange(TIMES, dtype=jnp.int32)[None, None, :]
    shift = ((frame - delay.T[:, :, None]) % TIMES).reshape(chans, TRIALS * TIMES)

    part = None
    for i, start in enumerate(starts):
        if i == len(starts) - 1:
            last, part = lax.optimization_barrier((spectra[-1], held))
            received.append(exchange(last))
            part = beam_stage(received[i - 1], gains, weights, shift, starts[i - 1], part)
        if i == len(starts) - 2:
            held = part
            continue
        part = beam_stage(received[i], gains, weights, shift, start, part)

    series = TRIALS * TIMES
    groups = [[x * cores + c for c in range(cores)] for x in range(grp_count // cores)]
    part = part.reshape(cores, BEAMS // cores, series)
    part = lax.all_to_all(
        part, "grp", split_axis=0, concat_axis=0, axis_index_groups=groups, tiled=True
    )
    part = jnp.sum(part.astype(jnp.float32), axis=0).astype(jnp.bfloat16)
    part = part.reshape(pairs * peers // cores, owned, series)
    groups = [
        [
            (p * grp_count + x * cores + c) * mem_count + m
            for p in range(pairs)
            for x in range(grp_count // cores)
            for m in range(mem_count)
        ]
        for c in range(cores)
    ]
    part = lax.all_to_all(
        part, ("pair",) + PEERS, split_axis=0, concat_axis=0, axis_index_groups=groups, tiled=True
    )
    series = jnp.sum(part.astype(jnp.float32), axis=0)
    return series.reshape(1, owned, TRIALS, TIMES)


def solution(mesh):
    return jax.shard_map(
        local,
        mesh=mesh,
        in_specs=(P(PEERS, "pair", None), P(None, None, "mem"), P(), P(), P(), P()),
        out_specs=P("pair", PEERS, None, None),
        check_vma=False,
    )
```

```python
import functools
import math

import jax
import jax.numpy as jnp
from jax import lax
from jax.experimental import pallas as pl
from jax.experimental.pallas import tpu as pltpu
from jax.sharding import PartitionSpec as P

NFFT = 2048
CHANS = 1024
TAPS = 4
CYL = 4
NS = 256
FEEDS = 1024
BEAMS = 1024
TIMES = 32
TRIALS = 32
PEERS = ("grp", "mem")
LANES = 128


def pfb_window(tap_count, length):
    offsets = jnp.arange(tap_count * length, dtype=jnp.float32) + 0.5
    shaped = jnp.sinc((offsets - tap_count * length / 2.0) / length)
    taper_term = 0.5 - 0.5 * jnp.cos(offsets * (2.0 * math.pi / (tap_count * length)))
    return (shaped * taper_term).reshape(tap_count, length)


def turn(index, length):
    angles = (index % length).astype(jnp.float32) * (2.0 * math.pi / length)
    return lax.optimization_barrier((jnp.cos(angles), jnp.sin(angles)))


def times(a, b):
    return (a[0] * b[0] - a[1] * b[1], a[0] * b[1] + a[1] * b[0])


def channel_table(chan_of, quarter):
    chan = chan_of[None, :]
    high = turn(jnp.arange(16, dtype=jnp.int32)[:, None] * 128 * chan, NFFT)
    mid = turn(jnp.arange(16, dtype=jnp.int32)[:, None] * 8 * chan, NFFT)
    low = turn(jnp.arange(8, dtype=jnp.int32)[:, None] * chan + quarter[None, :] * (NFFT // 4), NFFT)
    upper = times([p[:, None, :] for p in high], [p[None, :, :] for p in mid])
    upper = lax.optimization_barrier(tuple(p.reshape(NFFT // 8, 1, -1) for p in upper))
    table = upper[0] * low[0][None] - upper[1] * low[1][None]
    return table.astype(jnp.bfloat16).reshape(NFFT, -1)


def beam_weights(cylinder_map):
    slots = jnp.arange(FEEDS, dtype=jnp.int32)
    hit = cylinder_map[:, None] == slots[None, :]
    slot_of = jnp.sum(jnp.where(hit, slots[:, None], 0), axis=0)
    cyl, pos = slot_of // NS, slot_of % NS
    e = jnp.arange(CYL, dtype=jnp.int32).reshape(CYL, 1, 1)
    hh = jnp.arange(16, dtype=jnp.int32).reshape(1, 16, 1)
    upper = turn(16 * pos * hh + (NS // CYL) * e * cyl, NS)
    a = jnp.arange(2, dtype=jnp.int32).reshape(2, 1, 1)
    hl = jnp.arange(8, dtype=jnp.int32).reshape(1, 8, 1)
    lower = turn(pos * (2 * hl + a), NS)
    real, imag = times(
        [p[None, :, :, None, :] for p in upper], [p[:, None, None, :, :] for p in lower]
    )
    return jnp.concatenate(
        [p.astype(jnp.bfloat16).reshape(BEAMS, FEEDS) for p in (real, imag)], axis=1
    )


BEAM_VMEM = 40
DFT_VMEM = 40
CHUNKS = (8, 20, 4)


def dft_kernel(frames, feeds, window_ref, volt_ref, table_ref, out_ref, framed_ref):
    @pl.when(pl.program_id(0) == 0)
    def _():
        for t in range(frames):
            total = volt_ref[:, t * NFFT : (t + 1) * NFFT].astype(jnp.float32) * window_ref[0:1, :]
            for j in range(1, TAPS):
                tap = volt_ref[:, (t + j) * NFFT : (t + j + 1) * NFFT].astype(jnp.float32)
                total = total + tap * window_ref[j : j + 1, :]
            framed_ref[t * feeds : (t + 1) * feeds, :] = total.astype(jnp.bfloat16)

    part = jnp.dot(framed_ref[...], table_ref[...], preferred_element_type=jnp.float32)
    part = (part * (1.0 / math.sqrt(NFFT))).astype(jnp.bfloat16)
    for i in range(out_ref.shape[0]):
        out_ref[i] = part[:, i * LANES : (i + 1) * LANES].reshape(frames, feeds, LANES)


def dft_stage(voltages, window, table, start, frames, peers):
    feeds = voltages.shape[0]
    length = (frames + TAPS - 1) * NFFT
    volt = lax.slice_in_dim(voltages, start * NFFT, start * NFFT + length, axis=2)
    volt = volt.reshape(feeds, length)
    width = table.shape[1] // peers
    if width != LANES:
        view = volt.reshape(feeds, frames + TAPS - 1, NFFT).astype(jnp.float32)
        framed = view[:, 0:frames] * window[0]
        for j in range(1, TAPS):
            framed = framed + view[:, j : j + frames] * window[j]
        rows = jnp.swapaxes(framed.astype(jnp.bfloat16), 0, 1).reshape(frames * feeds, NFFT)
        part = jnp.dot(rows, table, preferred_element_type=jnp.float32) * (1.0 / math.sqrt(NFFT))
        part = part.astype(jnp.bfloat16).reshape(frames, feeds, peers, width)
        return jnp.moveaxis(part, 2, 0)
    step = 4
    return pl.pallas_call(
        functools.partial(dft_kernel, frames, feeds),
        grid=(peers // step,),
        out_shape=jax.ShapeDtypeStruct((peers, frames, feeds, width), jnp.bfloat16),
        in_specs=[
            pl.BlockSpec((TAPS, NFFT), lambda i: (0, 0)),
            pl.BlockSpec((feeds, length), lambda i: (0, 0)),
            pl.BlockSpec((NFFT, step * width), lambda i: (0, i)),
        ],
        out_specs=pl.BlockSpec((step, frames, feeds, width), lambda i: (i, 0, 0, 0)),
        scratch_shapes=[pltpu.VMEM((frames * feeds, NFFT), jnp.bfloat16)],
        compiler_params=pltpu.CompilerParams(
            dimension_semantics=("arbitrary",), vmem_limit_bytes=DFT_VMEM * 1024 * 1024
        ),
    )(window, volt, table)


HIT = (TIMES - 1) / (TIMES * TIMES)
MISS = -1.0 / (TIMES * TIMES)


def beam_kernel(start, frames, chans, r_ref, ga_ref, gb_ref, w_ref, e_ref, *rest):
    acc_ref = rest[0] if len(rest) == 6 else None
    out_ref, even_ref, odd_ref, t_ref, p_ref = rest[-5:]
    width = 2 * chans
    lane = lax.broadcasted_iota(jnp.int32, (FEEDS, width), 1)
    sign = jnp.where(lane < chans, 1.0, -1.0)
    low = lax.broadcasted_iota(jnp.int32, (BEAMS, width), 1) < chans

    def calibrate(pair, x_ref):
        for u in range(2):
            i = 2 * pair + u
            volt = r_ref[:, i].reshape(FEEDS, width).astype(jnp.float32)
            cal = volt * ga_ref[...] + pltpu.roll(volt, chans, 1) * gb_ref[...]
            turned = pltpu.roll(cal, chans, 1) * sign
            cols = slice(u * width, (u + 1) * width)
            x_ref[0:FEEDS, cols] = cal.astype(jnp.bfloat16)
            x_ref[FEEDS : 2 * FEEDS, cols] = turned.astype(jnp.bfloat16)
            hit = e_ref[...] == start + i
            rows = pl.ds(pl.multiple_of(i * chans, chans), chans)
            t_ref[rows, :] = jnp.where(hit, HIT, MISS).astype(jnp.bfloat16)

    def form(pair, x_ref):
        beams = jnp.dot(w_ref[...], x_ref[...], preferred_element_type=jnp.float32)
        squares = beams * beams
        one, two = squares[:, :width], squares[:, width:]
        first = one + pltpu.roll(one, chans, 1)
        second = two + pltpu.roll(two, chans, 1)
        power = jnp.where(low, first, second) * (1.0 / FEEDS)
        p_ref[:, pl.ds(pl.multiple_of(pair * width, width), width)] = power.astype(jnp.bfloat16)

    pairs = frames // 2
    calibrate(0, even_ref)

    def body(k, carry):
        form(2 * k, even_ref)
        calibrate(2 * k + 1, odd_ref)
        form(2 * k + 1, odd_ref)
        calibrate(jnp.minimum(2 * k + 2, pairs - 1), even_ref)
        return carry

    lax.fori_loop(0, pairs // 2, body, 0)
    if pairs % 2:
        form(pairs - 1, even_ref)
    part = jnp.dot(p_ref[...], t_ref[...], preferred_element_type=jnp.float32)
    if acc_ref is not None:
        part = part + acc_ref[...]
    out_ref[...] = part.astype(out_ref.dtype)


def beam_stage(received, gains, weights, shift, start, acc):
    _, frames, _, width = received.shape
    chans = width // 2
    last = start + frames == TIMES
    held = jnp.bfloat16 if last else jnp.float32
    if width != LANES:
        volt = jnp.moveaxis(received, 1, 0).reshape(frames, FEEDS, 2, chans).astype(jnp.float32)
        ga, gb = (g.reshape(FEEDS, 2, chans) for g in gains)
        cal = (volt * ga + volt[:, :, ::-1] * gb).astype(jnp.bfloat16)
        turned = jnp.stack([cal[:, :, 1], -cal[:, :, 0]], axis=2)
        both = jnp.concatenate([cal, turned], axis=1)
        beams = jnp.einsum("bf,tfrc->btrc", weights, both, preferred_element_type=jnp.float32)
        power = jnp.sum(beams * beams, axis=2) * (1.0 / FEEDS)
        power = power.astype(jnp.bfloat16).reshape(BEAMS, frames * chans)
        frame = start + jnp.arange(frames, dtype=jnp.int32)[:, None, None]
        spread = jnp.where(shift[None] == frame, HIT, MISS).astype(jnp.bfloat16)
        spread = spread.reshape(frames * chans, -1)
        part = jnp.dot(power, spread, preferred_element_type=jnp.float32)
        return (part if acc is None else part + acc).astype(held)
    series = TRIALS * TIMES
    operands = (received, *gains, weights, shift) + (() if acc is None else (acc,))
    return pl.pallas_call(
        functools.partial(beam_kernel, start, frames, chans),
        out_shape=jax.ShapeDtypeStruct((BEAMS, series), held),
        in_specs=[pl.BlockSpec(memory_space=pltpu.VMEM)] * len(operands),
        out_specs=pl.BlockSpec(memory_space=pltpu.VMEM),
        scratch_shapes=[
            pltpu.VMEM((2 * FEEDS, 2 * width), jnp.bfloat16),
            pltpu.VMEM((2 * FEEDS, 2 * width), jnp.bfloat16),
            pltpu.VMEM((frames * chans, series), jnp.bfloat16),
            pltpu.VMEM((BEAMS, frames * chans), jnp.bfloat16),
        ],
        compiler_params=pltpu.CompilerParams(vmem_limit_bytes=BEAM_VMEM * 1024 * 1024),
    )(*operands)


def local(voltages, gain_table, gain_index, cylinder_map, delays, chan_map):
    feeds = voltages.shape[0]
    grp_count, mem_count = lax.axis_size("grp"), lax.axis_size("mem")
    peers = grp_count * mem_count
    chans = CHANS // peers
    grp, mem = lax.axis_index("grp"), lax.axis_index("mem")

    window = pfb_window(TAPS, NFFT)
    peer = jnp.arange(peers, dtype=jnp.int32)
    base = peer % mem_count * (CHANS // mem_count) + peer // mem_count * chans
    chan_of = base[:, None, None] + jnp.arange(chans, dtype=jnp.int32)[None, None, :]
    quarter = jnp.arange(2, dtype=jnp.int32)[None, :, None]
    chan_of, quarter = (
        jnp.broadcast_to(v, (peers, 2, chans)).reshape(-1) for v in (chan_of, quarter)
    )
    table = channel_table(chan_of, quarter)

    table = lax.optimization_barrier(table)
    starts = [sum(CHUNKS[:i]) for i in range(len(CHUNKS))]

    def exchange(spectra):
        return lax.all_to_all(spectra, PEERS, split_axis=0, concat_axis=0, tiled=True)

    spectra = [
        dft_stage(voltages, window, table, start, frames, peers)
        for start, frames in zip(starts, CHUNKS)
    ]
    received = [exchange(block) for block in spectra[:-1]]

    pairs = lax.axis_size("pair")
    cores = 2 if grp_count % 2 == 0 else 1
    owned = BEAMS // (pairs * peers)
    weights = beam_weights(cylinder_map)
    weights = weights.reshape(pairs, grp_count // cores, cores, mem_count * owned, 2 * FEEDS)
    weights = jnp.moveaxis(weights, 2, 0).reshape(BEAMS, 2 * FEEDS)
    gain_here = lax.dynamic_slice_in_dim(gain_table, grp * chans, chans, 2)
    gain_rows = gain_index[:, lax.axis_index("pair")]
    pick = gain_rows[:, None] == jnp.arange(gain_table.shape[0], dtype=jnp.int32)[None, :]
    gain_values = jnp.dot(
        pick.astype(jnp.float32),
        gain_here.reshape(gain_table.shape[0], 2 * chans),
        precision=lax.Precision.HIGHEST,
    )
    gain_real, gain_imag = gain_values[:, :chans], gain_values[:, chans:]
    gains = (
        jnp.concatenate([gain_real, gain_real], axis=1),
        jnp.concatenate([-gain_imag, gain_imag], axis=1),
    )

    first = mem * (CHANS // mem_count) + grp * chans
    freq = lax.dynamic_slice_in_dim(chan_map, first, chans, 0)
    column = jnp.arange(CHANS, dtype=jnp.int32)[:, None] == freq[None, :]
    delay = jnp.dot(
        delays.astype(jnp.bfloat16), column.astype(jnp.bfloat16), preferred_element_type=jnp.float32
    ).astype(jnp.int32)
    frame = jnp.arange(TIMES, dtype=jnp.int32)[None, None, :]
    shift = ((frame - delay.T[:, :, None]) % TIMES).reshape(chans, TRIALS * TIMES)

    part = None
    for i, start in enumerate(starts):
        if i == len(starts) - 1:
            last, part = lax.optimization_barrier((spectra[-1], held))
            received.append(exchange(last))
            part = beam_stage(received[i - 1], gains, weights, shift, starts[i - 1], part)
        if i == len(starts) - 2:
            held = part
            continue
        part = beam_stage(received[i], gains, weights, shift, start, part)

    series = TRIALS * TIMES
    groups = [[x * cores + c for c in range(cores)] for x in range(grp_count // cores)]
    part = part.reshape(cores, BEAMS // cores, series)
    part = lax.all_to_all(
        part, "grp", split_axis=0, concat_axis=0, axis_index_groups=groups, tiled=True
    )
    part = jnp.sum(part.astype(jnp.float32), axis=0).astype(jnp.bfloat16)
    part = part.reshape(pairs * peers // cores, owned, series)
    groups = [
        [
            (p * grp_count + x * cores + c) * mem_count + m
            for p in range(pairs)
            for x in range(grp_count // cores)
            for m in range(mem_count)
        ]
        for c in range(cores)
    ]
    part = lax.all_to_all(
        part, ("pair",) + PEERS, split_axis=0, concat_axis=0, axis_index_groups=groups, tiled=True
    )
    series = jnp.sum(part.astype(jnp.float32), axis=0)
    return series.reshape(1, owned, TRIALS, TIMES)


def solution(mesh):
    return jax.shard_map(
        local,
        mesh=mesh,
        in_specs=(P(PEERS, "pair", None), P(None, None, "mem"), P(), P(), P(), P()),
        out_specs=P("pair", PEERS, None, None),
        check_vma=False,
    )
```

```python
import functools
import math

import jax
import jax.numpy as jnp
from jax import lax
from jax.experimental import pallas as pl
from jax.experimental.pallas import tpu as pltpu
from jax.sharding import PartitionSpec as P

NFFT = 2048
CHANS = 1024
TAPS = 4
CYL = 4
NS = 256
FEEDS = 1024
BEAMS = 1024
TIMES = 32
TRIALS = 32
PEERS = ("grp", "mem")
LANES = 128


def pfb_window(tap_count, length):
    offsets = jnp.arange(tap_count * length, dtype=jnp.float32) + 0.5
    shaped = jnp.sinc((offsets - tap_count * length / 2.0) / length)
    taper_term = 0.5 - 0.5 * jnp.cos(offsets * (2.0 * math.pi / (tap_count * length)))
    return (shaped * taper_term).reshape(tap_count, length)


def turn(index, length):
    angles = (index % length).astype(jnp.float32) * (2.0 * math.pi / length)
    return lax.optimization_barrier((jnp.cos(angles), jnp.sin(angles)))


def times(a, b):
    return (a[0] * b[0] - a[1] * b[1], a[0] * b[1] + a[1] * b[0])


def channel_table(chan_of, quarter):
    chan = chan_of[None, :]
    high = turn(jnp.arange(16, dtype=jnp.int32)[:, None] * 128 * chan, NFFT)
    mid = turn(jnp.arange(16, dtype=jnp.int32)[:, None] * 8 * chan, NFFT)
    low = turn(jnp.arange(8, dtype=jnp.int32)[:, None] * chan + quarter[None, :] * (NFFT // 4), NFFT)
    upper = times([p[:, None, :] for p in high], [p[None, :, :] for p in mid])
    upper = lax.optimization_barrier(tuple(p.reshape(NFFT // 8, 1, -1) for p in upper))
    table = upper[0] * low[0][None] - upper[1] * low[1][None]
    return table.astype(jnp.bfloat16).reshape(NFFT, -1)


def beam_weights(cylinder_map):
    slots = jnp.arange(FEEDS, dtype=jnp.int32)
    hit = cylinder_map[:, None] == slots[None, :]
    slot_of = jnp.sum(jnp.where(hit, slots[:, None], 0), axis=0)
    cyl, pos = slot_of // NS, slot_of % NS
    e = jnp.arange(CYL, dtype=jnp.int32).reshape(CYL, 1, 1)
    hh = jnp.arange(16, dtype=jnp.int32).reshape(1, 16, 1)
    upper = turn(16 * pos * hh + (NS // CYL) * e * cyl, NS)
    a = jnp.arange(2, dtype=jnp.int32).reshape(2, 1, 1)
    hl = jnp.arange(8, dtype=jnp.int32).reshape(1, 8, 1)
    lower = turn(pos * (2 * hl + a), NS)
    real, imag = times(
        [p[None, :, :, None, :] for p in upper], [p[:, None, None, :, :] for p in lower]
    )
    return jnp.concatenate(
        [p.astype(jnp.bfloat16).reshape(BEAMS, FEEDS) for p in (real, imag)], axis=1
    )


BEAM_VMEM = 40
DFT_VMEM = 40
CHUNKS = (4, 24, 4)


def dft_kernel(frames, feeds, window_ref, volt_ref, table_ref, out_ref, framed_ref):
    @pl.when(pl.program_id(0) == 0)
    def _():
        for t in range(frames):
            total = volt_ref[:, t * NFFT : (t + 1) * NFFT].astype(jnp.float32) * window_ref[0:1, :]
            for j in range(1, TAPS):
                tap = volt_ref[:, (t + j) * NFFT : (t + j + 1) * NFFT].astype(jnp.float32)
                total = total + tap * window_ref[j : j + 1, :]
            framed_ref[t * feeds : (t + 1) * feeds, :] = total.astype(jnp.bfloat16)

    part = jnp.dot(framed_ref[...], table_ref[...], preferred_element_type=jnp.float32)
    part = (part * (1.0 / math.sqrt(NFFT))).astype(jnp.bfloat16)
    for i in range(out_ref.shape[0]):
        out_ref[i] = part[:, i * LANES : (i + 1) * LANES].reshape(frames, feeds, LANES)


def dft_stage(voltages, window, table, start, frames, peers):
    feeds = voltages.shape[0]
    length = (frames + TAPS - 1) * NFFT
    volt = lax.slice_in_dim(voltages, start * NFFT, start * NFFT + length, axis=2)
    volt = volt.reshape(feeds, length)
    width = table.shape[1] // peers
    if width != LANES:
        view = volt.reshape(feeds, frames + TAPS - 1, NFFT).astype(jnp.float32)
        framed = view[:, 0:frames] * window[0]
        for j in range(1, TAPS):
            framed = framed + view[:, j : j + frames] * window[j]
        rows = jnp.swapaxes(framed.astype(jnp.bfloat16), 0, 1).reshape(frames * feeds, NFFT)
        part = jnp.dot(rows, table, preferred_element_type=jnp.float32) * (1.0 / math.sqrt(NFFT))
        part = part.astype(jnp.bfloat16).reshape(frames, feeds, peers, width)
        return jnp.moveaxis(part, 2, 0)
    step = 4
    return pl.pallas_call(
        functools.partial(dft_kernel, frames, feeds),
        grid=(peers // step,),
        out_shape=pltpu.HBM((peers, frames, feeds, width), jnp.bfloat16),
        in_specs=[
            pl.BlockSpec((TAPS, NFFT), lambda i: (0, 0)),
            pl.BlockSpec((feeds, length), lambda i: (0, 0)),
            pl.BlockSpec((NFFT, step * width), lambda i: (0, i)),
        ],
        out_specs=pl.BlockSpec((step, frames, feeds, width), lambda i: (i, 0, 0, 0)),
        scratch_shapes=[pltpu.VMEM((frames * feeds, NFFT), jnp.bfloat16)],
        compiler_params=pltpu.CompilerParams(
            dimension_semantics=("arbitrary",), vmem_limit_bytes=DFT_VMEM * 1024 * 1024
        ),
    )(window, volt, table)


HIT = (TIMES - 1) / (TIMES * TIMES)
MISS = -1.0 / (TIMES * TIMES)


def beam_kernel(start, frames, chans, r_ref, ga_ref, gb_ref, w_ref, e_ref, *rest):
    acc_ref = rest[0] if len(rest) == 6 else None
    out_ref, even_ref, odd_ref, t_ref, p_ref = rest[-5:]
    width = 2 * chans
    lane = lax.broadcasted_iota(jnp.int32, (FEEDS, width), 1)
    sign = jnp.where(lane < chans, 1.0, -1.0)
    low = lax.broadcasted_iota(jnp.int32, (BEAMS, width), 1) < chans

    def calibrate(pair, x_ref):
        for u in range(2):
            i = 2 * pair + u
            volt = r_ref[:, i].reshape(FEEDS, width).astype(jnp.float32)
            cal = volt * ga_ref[...] + pltpu.roll(volt, chans, 1) * gb_ref[...]
            turned = pltpu.roll(cal, chans, 1) * sign
            cols = slice(u * width, (u + 1) * width)
            x_ref[0:FEEDS, cols] = cal.astype(jnp.bfloat16)
            x_ref[FEEDS : 2 * FEEDS, cols] = turned.astype(jnp.bfloat16)
            hit = e_ref[...] == start + i
            rows = pl.ds(pl.multiple_of(i * chans, chans), chans)
            t_ref[rows, :] = jnp.where(hit, HIT, MISS).astype(jnp.bfloat16)

    def form(pair, x_ref):
        beams = jnp.dot(w_ref[...], x_ref[...], preferred_element_type=jnp.float32)
        squares = beams * beams
        one, two = squares[:, :width], squares[:, width:]
        first = one + pltpu.roll(one, chans, 1)
        second = two + pltpu.roll(two, chans, 1)
        power = jnp.where(low, first, second) * (1.0 / FEEDS)
        p_ref[:, pl.ds(pl.multiple_of(pair * width, width), width)] = power.astype(jnp.bfloat16)

    pairs = frames // 2
    calibrate(0, even_ref)

    def body(k, carry):
        form(2 * k, even_ref)
        calibrate(2 * k + 1, odd_ref)
        form(2 * k + 1, odd_ref)
        calibrate(jnp.minimum(2 * k + 2, pairs - 1), even_ref)
        return carry

    lax.fori_loop(0, pairs // 2, body, 0)
    if pairs % 2:
        form(pairs - 1, even_ref)
    part = jnp.dot(p_ref[...], t_ref[...], preferred_element_type=jnp.float32)
    if acc_ref is not None:
        part = part + acc_ref[...]
    out_ref[...] = part.astype(out_ref.dtype)


def beam_stage(received, gains, weights, shift, start, acc):
    _, frames, _, width = received.shape
    chans = width // 2
    last = start + frames == TIMES
    held = jnp.bfloat16 if last else jnp.float32
    if width != LANES:
        volt = jnp.moveaxis(received, 1, 0).reshape(frames, FEEDS, 2, chans).astype(jnp.float32)
        ga, gb = (g.reshape(FEEDS, 2, chans) for g in gains)
        cal = (volt * ga + volt[:, :, ::-1] * gb).astype(jnp.bfloat16)
        turned = jnp.stack([cal[:, :, 1], -cal[:, :, 0]], axis=2)
        both = jnp.concatenate([cal, turned], axis=1)
        beams = jnp.einsum("bf,tfrc->btrc", weights, both, preferred_element_type=jnp.float32)
        power = jnp.sum(beams * beams, axis=2) * (1.0 / FEEDS)
        power = power.astype(jnp.bfloat16).reshape(BEAMS, frames * chans)
        frame = start + jnp.arange(frames, dtype=jnp.int32)[:, None, None]
        spread = jnp.where(shift[None] == frame, HIT, MISS).astype(jnp.bfloat16)
        spread = spread.reshape(frames * chans, -1)
        part = jnp.dot(power, spread, preferred_element_type=jnp.float32)
        return (part if acc is None else part + acc).astype(held)
    series = TRIALS * TIMES
    operands = (received, *gains, weights, shift) + (() if acc is None else (acc,))
    return pl.pallas_call(
        functools.partial(beam_kernel, start, frames, chans),
        out_shape=jax.ShapeDtypeStruct((BEAMS, series), held),
        in_specs=[pl.BlockSpec(memory_space=pltpu.VMEM)] * len(operands),
        out_specs=pl.BlockSpec(memory_space=pltpu.VMEM),
        scratch_shapes=[
            pltpu.VMEM((2 * FEEDS, 2 * width), jnp.bfloat16),
            pltpu.VMEM((2 * FEEDS, 2 * width), jnp.bfloat16),
            pltpu.VMEM((frames * chans, series), jnp.bfloat16),
            pltpu.VMEM((BEAMS, frames * chans), jnp.bfloat16),
        ],
        compiler_params=pltpu.CompilerParams(vmem_limit_bytes=BEAM_VMEM * 1024 * 1024),
    )(*operands)


def local(voltages, gain_table, gain_index, cylinder_map, delays, chan_map):
    feeds = voltages.shape[0]
    grp_count, mem_count = lax.axis_size("grp"), lax.axis_size("mem")
    peers = grp_count * mem_count
    chans = CHANS // peers
    grp, mem = lax.axis_index("grp"), lax.axis_index("mem")

    window = pfb_window(TAPS, NFFT)
    peer = jnp.arange(peers, dtype=jnp.int32)
    base = peer % mem_count * (CHANS // mem_count) + peer // mem_count * chans
    chan_of = base[:, None, None] + jnp.arange(chans, dtype=jnp.int32)[None, None, :]
    quarter = jnp.arange(2, dtype=jnp.int32)[None, :, None]
    chan_of, quarter = (
        jnp.broadcast_to(v, (peers, 2, chans)).reshape(-1) for v in (chan_of, quarter)
    )
    table = channel_table(chan_of, quarter)

    table = lax.optimization_barrier(table)
    starts = [sum(CHUNKS[:i]) for i in range(len(CHUNKS))]

    def exchange(spectra):
        return lax.all_to_all(spectra, PEERS, split_axis=0, concat_axis=0, tiled=True)

    spectra = [
        dft_stage(voltages, window, table, start, frames, peers)
        for start, frames in zip(starts, CHUNKS)
    ]
    received = [exchange(block) for block in spectra[:-1]]

    pairs = lax.axis_size("pair")
    cores = 2 if grp_count % 2 == 0 else 1
    owned = BEAMS // (pairs * peers)
    weights = beam_weights(cylinder_map)
    weights = weights.reshape(pairs, grp_count // cores, cores, mem_count * owned, 2 * FEEDS)
    weights = jnp.moveaxis(weights, 2, 0).reshape(BEAMS, 2 * FEEDS)
    gain_here = lax.dynamic_slice_in_dim(gain_table, grp * chans, chans, 2)
    gain_rows = gain_index[:, lax.axis_index("pair")]
    pick = gain_rows[:, None] == jnp.arange(gain_table.shape[0], dtype=jnp.int32)[None, :]
    gain_values = jnp.dot(
        pick.astype(jnp.float32),
        gain_here.reshape(gain_table.shape[0], 2 * chans),
        precision=lax.Precision.HIGHEST,
    )
    gain_real, gain_imag = gain_values[:, :chans], gain_values[:, chans:]
    gains = (
        jnp.concatenate([gain_real, gain_real], axis=1),
        jnp.concatenate([-gain_imag, gain_imag], axis=1),
    )

    first = mem * (CHANS // mem_count) + grp * chans
    freq = lax.dynamic_slice_in_dim(chan_map, first, chans, 0)
    column = jnp.arange(CHANS, dtype=jnp.int32)[:, None] == freq[None, :]
    delay = jnp.dot(
        delays.astype(jnp.bfloat16), column.astype(jnp.bfloat16), preferred_element_type=jnp.float32
    ).astype(jnp.int32)
    frame = jnp.arange(TIMES, dtype=jnp.int32)[None, None, :]
    shift = ((frame - delay.T[:, :, None]) % TIMES).reshape(chans, TRIALS * TIMES)

    part = None
    for i, start in enumerate(starts):
        if i == len(starts) - 1:
            last, part = lax.optimization_barrier((spectra[-1], held))
            received.append(exchange(last))
            part = beam_stage(received[i - 1], gains, weights, shift, starts[i - 1], part)
        if i == len(starts) - 2:
            held = part
            continue
        part = beam_stage(received[i], gains, weights, shift, start, part)

    series = TRIALS * TIMES
    groups = [[x * cores + c for c in range(cores)] for x in range(grp_count // cores)]
    part = part.reshape(cores, BEAMS // cores, series)
    part = lax.all_to_all(
        part, "grp", split_axis=0, concat_axis=0, axis_index_groups=groups, tiled=True
    )
    part = jnp.sum(part.astype(jnp.float32), axis=0).astype(jnp.bfloat16)
    part = part.reshape(pairs * peers // cores, owned, series)
    groups = [
        [
            (p * grp_count + x * cores + c) * mem_count + m
            for p in range(pairs)
            for x in range(grp_count // cores)
            for m in range(mem_count)
        ]
        for c in range(cores)
    ]
    part = lax.all_to_all(
        part, ("pair",) + PEERS, split_axis=0, concat_axis=0, axis_index_groups=groups, tiled=True
    )
    series = jnp.sum(part.astype(jnp.float32), axis=0)
    return series.reshape(1, owned, TRIALS, TIMES)


def solution(mesh):
    return jax.shard_map(
        local,
        mesh=mesh,
        in_specs=(P(PEERS, "pair", None), P(None, None, "mem"), P(), P(), P(), P()),
        out_specs=P("pair", PEERS, None, None),
        check_vma=False,
    )
```
